32 devices in a mesh: gx: 2 (over y), gy: 4 (over x, core), gz: 4 (over z).
Axes of the slice: x: 2, y: 2, z: 4, core: 2. Of those that a mesh axis runs over, the one named last changes fastest.
Arguments:
- displacement: float32 [3, 4, 16, 512], P(None, 'gx', 'gy', 'gz'), may hold values from -0.4 to 0.4
- load: float32 [3, 4, 16, 512], P(None, 'gx', 'gy', 'gz'), may hold values from -12 to 12
- material: int32 [4, 16, 512], P('gx', 'gy', 'gz'), may hold values from 0 to 7, as said below
- free_node: int32 [4, 16, 512], P('gx', 'gy', 'gz'), may hold values 0 or 1
- table: float32 [8, 3], replicated, may hold values from 0.5 to 20, as said below
Outputs:
- increment: float32 [3, 4, 16, 512], P(None, 'gx', 'gy', 'gz')
- residual: float32 [3, 4, 16, 512], P(None, 'gx', 'gy', 'gz')
The draws below stay inside these ranges and needn't reach their ends.
Inputs may be any that keep to these rules, and one draw needn't show every extreme that they name: The material id of an element with third index k lies between band and band + 2, where band = (k * 6) // 512. `table`: all entries positive.
All inputs are finite; a program needn't handle non-finite values. No bound on the sum of `free_node` on one device may be relied on, other than what follows from the above.
Results may differ from the reference program's by a relative error of at most 0.0004.
Values sent between devices are 32-bit elements; how exact they have to be, the bound alone decides.
A program may use at most 64 MiB of HBM per device.

```python
import jax
import jax.numpy as jnp

NMAT = 8
OUTER = 2
NX = 4
NY = 16
NZ = 512


def draw_material(key, part):
    depth = jnp.arange(NZ, dtype=jnp.int32)
    band = depth * (NMAT - 2) // NZ
    offset = jax.random.randint(key, (NX, NY, NZ), 0, 3)
    return (band[None, None, :] + offset).astype(jnp.int32)


def draw_table(key, part):
    rows = jnp.arange(NMAT, dtype=jnp.float32)
    base = jnp.exp(rows * (jnp.log(3.0) / (NMAT - 1)))
    jitter = jnp.exp(jax.random.uniform(key, (NMAT, 3), jnp.float32, -0.4, 0.4))
    scale = jnp.array([1.0, 1.0, 4.0], jnp.float32)
    return (base[:, None] * jitter * scale[None, :]).astype(jnp.float32)


def place_ends(drawn, stream_key, low, top_value):
    place = [jax.random.randint(jax.random.fold_in(stream_key, axis), (), 0, length) for axis, length in enumerate(drawn.shape)]
    longest = drawn.shape.index(max(drawn.shape))
    neighbour = place[:longest] + [(place[longest] + 1) % drawn.shape[longest]] + place[longest + 1:]
    return drawn.at[tuple(place)].set(low).at[tuple(neighbour)].set(top_value)


def block_scale(key, dims, shards, low, largest):
    level, own = 1.0, jax.random.fold_in(key, 6)
    for position, parts in shards:
        heights = jnp.exp(jax.random.uniform(jax.random.fold_in(own, position), (parts,), jnp.float32, low / len(shards), largest / len(shards)))
        level = level * jnp.repeat(heights, dims[position] // parts).reshape([-1 if axis == position else 1 for axis in range(len(dims))])
    return level


def bell_draw(stream_key, extent, width, most, cuts=(), kind=jnp.bfloat16):
    factor_of = block_scale(stream_key, extent, cuts, -0.22, 0.18) if cuts else 1.0
    result = jax.random.normal(stream_key, extent, jnp.float32) * width * factor_of
    return jnp.minimum(jnp.maximum(result, -most), most).astype(kind)


def setup_inputs(seed: int = 0) -> dict:
    keys = jax.random.split(jax.random.key(seed), 6)
    return {
        "displacement": bell_draw(keys[0], (3, NX, NY, NZ), 0.08, 0.4, ((1, 2), (2, 4), (3, 4)), jnp.float32),
        "load": bell_draw(keys[1], (3, NX, NY, NZ), 2.0, 12.0, ((1, 2), (2, 4), (3, 4)), jnp.float32),
        "material": draw_material(jax.random.fold_in(keys[5], 71), 0),
        "free_node": place_ends((jax.random.randint(keys[3], (NX, NY, NZ), 0, 8) < 7).astype(jnp.int32), jax.random.fold_in(keys[3], 1), 0, 1),
        "table": draw_table(jax.random.fold_in(keys[5], 71), 0),
    }


CORNERS = [(a, b, c) for a in (0, 1) for b in (0, 1) for c in (0, 1)]
SHIFTS = (9.6, 51.4)
HALF_WIDTH = 29.5

def slopes(corner):
    return [0.25 * (2 * corner[d] - 1) for d in range(3)]

def gradient_tensor(pieces):
    return [[sum((pieces[n][i] * slopes(CORNERS[n])[j] for n in range(8))) for j in range(3)] for i in range(3)]

def material_state(grad, lame_first, shear):
    frame = [[grad[i][j] + (1.0 if i == j else 0.0) for j in range(3)] for i in range(3)]
    strain = [[0.5 * (sum((frame[k][i] * frame[k][j] for k in range(3))) - (1.0 if i == j else 0.0)) for j in range(3)] for i in range(3)]
    trace = strain[0][0] + strain[1][1] + strain[2][2]
    stress = [[2.0 * shear * strain[i][j] + (lame_first * trace if i == j else 0.0) for j in range(3)] for i in range(3)]
    left = [[sum((frame[i][j] * frame[k][j] for j in range(3))) for k in range(3)] for i in range(3)]
    return (frame, stress, left)

def lookup(material, table):
    columns = [jnp.zeros(material.shape, jnp.float32) for column in range(3)]
    for row in range(table.shape[0]):
        hit = material == row
        columns = [jnp.where(hit, table[row, column], columns[column]) for column in range(3)]
    return columns

def element_view(field, corner):
    return field[..., corner[0]:corner[0] + NX - 1, corner[1]:corner[1] + NY - 1, corner[2]:corner[2] + NZ - 1]

def operate(vector, free, state):
    frame, stress, left, lame_first, shear, mass = state
    masked = vector * free
    pieces = [element_view(masked, corner) for corner in CORNERS]
    grad = gradient_tensor(pieces)
    trace = sum((frame[k][j] * grad[k][j] for k in range(3) for j in range(3)))
    left_grad = [[sum((left[i][k] * grad[k][j] for k in range(3))) for j in range(3)] for i in range(3)]
    cross = [[sum((grad[l][k] * frame[l][j] for l in range(3))) for j in range(3)] for k in range(3)]
    twisted = [[sum((frame[i][k] * cross[k][j] for k in range(3))) for j in range(3)] for i in range(3)]
    curved = [[sum((grad[i][l] * stress[l][j] for l in range(3))) for j in range(3)] for i in range(3)]
    piola = [[lame_first * trace * frame[i][j] + shear * (left_grad[i][j] + twisted[i][j]) + curved[i][j] for j in range(3)] for i in range(3)]
    output = jnp.zeros_like(vector)
    for n, corner in enumerate(CORNERS):
        slope = slopes(corner)
        term = jnp.stack([sum((piola[i][j] * slope[j] for j in range(3))) + 0.125 * mass * pieces[n][i] for i in range(3)])
        output = output.at[:, corner[0]:corner[0] + NX - 1, corner[1]:corner[1] + NY - 1, corner[2]:corner[2] + NZ - 1].add(term)
    return free * output + (1.0 - free) * vector

def solve_small(matrix, vector):
    sym = 0.5 * (matrix + matrix.T)
    l00 = jnp.sqrt(sym[0, 0])
    l10 = sym[1, 0] / l00
    l20 = sym[2, 0] / l00
    l11 = jnp.sqrt(sym[1, 1] - l10 * l10)
    l21 = (sym[2, 1] - l20 * l10) / l11
    l22 = jnp.sqrt(sym[2, 2] - l20 * l20 - l21 * l21)
    y0 = vector[0] / l00
    y1 = (vector[1] - l10 * y0) / l11
    y2 = (vector[2] - l20 * y0 - l21 * y1) / l22
    c2 = y2 / l22
    c1 = (y1 - l21 * c2) / l11
    c0 = (y0 - l10 * c1 - l20 * c2) / l00
    return [c0, c1, c2]

def reference(displacement, load, material, free_node, table):
    elements = material[:NX - 1, :NY - 1, :NZ - 1]
    lame_first, shear, mass = lookup(elements, table)
    pieces = [element_view(displacement, corner) for corner in CORNERS]
    frame, stress, left = material_state(gradient_tensor(pieces), lame_first, shear)
    state = (frame, stress, left, lame_first, shear, mass)
    free = free_node.astype(jnp.float32)
    residual = load * free
    increment = jnp.zeros_like(residual)
    for outer in range(OUTER):
        basis = [residual]
        images = []
        for step in range(3):
            images.append(operate(basis[step], free, state))
            if step < 2:
                basis.append((images[step] - SHIFTS[step] * basis[step]) / HALF_WIDTH)
        matrix = jnp.stack([jnp.stack([jnp.sum(basis[i] * images[j]) for j in range(3)]) for i in range(3)])
        vector = jnp.stack([jnp.sum(basis[i] * residual) for i in range(3)])
        coeffs = solve_small(matrix, vector)
        increment = increment + sum((coeffs[j] * basis[j] for j in range(3)))
        residual = residual - sum((coeffs[j] * images[j] for j in range(3)))
    return (increment, residual)
```

```python
import functools

import jax
import jax.numpy as jnp
from jax import lax
from jax.experimental import pallas as pl
from jax.experimental.pallas import tpu as pltpu
from jax.sharding import PartitionSpec as P

OUTER = 2
SHIFTS = (9.6, 51.4)
HALF_WIDTH = 29.5
FIELDS = 8
STRIP = 16
ROWS = 16
MESH = pl.DeviceIdType.MESH


def loop(count, body):
    if count <= 8:
        for i in range(count):
            body(i)
    else:

        def step(i, carry):
            body(i)
            return carry

        lax.fori_loop(0, count, step, 0)


def when(condition, body):
    pl.when(condition)(body)


def solve_small(gram, right):
    sym = [[0.5 * (gram[i][j] + gram[j][i]) for j in range(3)] for i in range(3)]
    l00 = jnp.sqrt(sym[0][0])
    l10 = sym[1][0] / l00
    l20 = sym[2][0] / l00
    l11 = jnp.sqrt(sym[1][1] - l10 * l10)
    l21 = (sym[2][1] - l20 * l10) / l11
    l22 = jnp.sqrt(sym[2][2] - l20 * l20 - l21 * l21)
    y0 = right[0] / l00
    y1 = (right[1] - l10 * y0) / l11
    y2 = (right[2] - l20 * y0 - l21 * y1) / l22
    c2 = y2 / l22
    c1 = (y1 - l21 * c2) / l11
    c0 = (y0 - l10 * c1 - l20 * c2) / l00
    return [c0, c1, c2]


def kernel(
    grid,
    shard,
    disp_ref,
    load_ref,
    mat_ref,
    free_ref,
    table_ref,
    inc_ref,
    res_ref,
    blocks,
    from_low,
    from_high,
    to_low,
    to_high,
    basis,
    image,
    nodal,
    piola,
    state,
    freeb,
    massb,
    own,
    sums,
    send_sem,
    recv_sem,
    sum_send,
    sum_recv,
):
    ngx, ngy, ngz = grid
    sx, sy, sz = shard
    nx, ny, nz = ngx * sx, ngy * sy, ngz * sz
    width = sz + 128
    n = ngx * ngy
    gx, gy, gz = lax.axis_index("gx"), lax.axis_index("gy"), lax.axis_index("gz")
    me = gx * ngy + gy
    has_low, has_high = gz > 0, gz < ngz - 1

    def target(p, z):
        return {"gx": p // ngy, "gy": lax.rem(p, ngy), "gz": z}

    barrier = pltpu.get_barrier_semaphore()

    def greet(p, z):
        pl.semaphore_signal(barrier, inc=1, device_id=target(p, z), device_id_type=MESH)

    def peers(count, first, body):
        loop(count, lambda k: body(lax.rem(me + first + k, n)))

    peers(n - 1, 1, lambda p: greet(p, gz))
    when(has_low, lambda: peers(n, 0, lambda p: greet(p, gz - 1)))
    when(has_high, lambda: peers(n, 0, lambda p: greet(p, gz + 1)))
    for z in range(ngz):
        when((z > gz + 1) | (z < gz - 1), lambda z=z: greet(me, z))

    for c in range(3):
        blocks[me, c] = disp_ref[c]
        blocks[me, 3 + c] = load_ref[c]
    blocks[me, 6] = mat_ref[...].astype(jnp.float32)
    blocks[me, 7] = free_ref[...].astype(jnp.float32)
    lane = lax.broadcasted_iota(jnp.int32, (sy, 128), 1)
    for i in range(sx):
        low = jnp.zeros((sy, 128), jnp.float32)
        high = jnp.zeros((sy, 128), jnp.float32)
        for f in range(FIELDS):
            if f < 3:
                part = disp_ref[f, i]
            elif f < 6:
                part = load_ref[f - 3, i]
            else:
                part = (mat_ref if f == 6 else free_ref)[i].astype(jnp.float32)
            here = (lane >= STRIP * f) & (lane < STRIP * (f + 1))
            first, last = part[:, :128], part[:, sz - 128 :]
            if f:
                first = pltpu.roll(first, STRIP * f, 1)
            if f < 7:
                last = pltpu.roll(last, STRIP * f + STRIP, 1)
            low = jnp.where(here, first, low)
            high = jnp.where(here, last, high)
        to_low[i] = low
        to_high[i] = high

    def clear(ref):
        ref[...] = jnp.zeros(ref.shape, jnp.float32)

    when(jnp.logical_not(has_low), lambda: clear(from_low))
    when(jnp.logical_not(has_high), lambda: clear(from_high))

    expected = n - 1 + jnp.where(has_low, n, 0) + jnp.where(has_high, n, 0)
    for z in range(ngz):
        expected = expected + jnp.where((z > gz + 1) | (z < gz - 1), 1, 0)
    pl.semaphore_wait(barrier, expected)

    def send(src, dst, slot, p, z):
        pltpu.make_async_remote_copy(
            src_ref=src,
            dst_ref=dst,
            send_sem=send_sem.at[slot],
            recv_sem=recv_sem.at[slot],
            device_id=target(p, z),
            device_id_type=MESH,
        ).start()

    peers(n - 1, 1, lambda p: send(blocks.at[me], blocks.at[me], 0, p, gz))
    when(
        has_high,
        lambda: peers(n, 0, lambda p: send(to_high, from_low.at[me], 1, p, gz + 1)),
    )
    when(
        has_low,
        lambda: peers(n, 0, lambda p: send(to_low, from_high.at[me], 2, p, gz - 1)),
    )

    def settle(ref, sem):
        pltpu.make_async_copy(ref, ref, sem).wait()

    for e in range(9):
        piola[e, 0] = jnp.zeros((ny, width), jnp.float32)
        piola[e, nx] = jnp.zeros((ny, width), jnp.float32)

    settle(blocks.at[pl.ds(0, n - 1)], recv_sem.at[0])
    when(has_low, lambda: settle(from_low, recv_sem.at[1]))
    when(has_high, lambda: settle(from_high, recv_sem.at[2]))

    tail = lax.broadcasted_iota(jnp.int32, (ny, 128), 1)

    def rows(ref, index, x):
        gi, i = x // sx, lax.rem(x, sx) if not isinstance(x, int) else x % sx
        return jnp.concatenate([ref[(gi * ngy + g,) + index + (i,)] for g in range(ngy)], axis=0)

    def whole_rows(f, x, after, before):
        up = after if f == 0 else pltpu.roll(after, 128 - STRIP * f, 1)
        down = before if f == 7 else pltpu.roll(before, 128 - STRIP - STRIP * f, 1)
        halo = jnp.where(tail < STRIP, up, jnp.where(tail >= 128 - STRIP, down, 0.0))
        return jnp.concatenate([rows(blocks, (f,), x), halo], axis=1)

    def unpack(x):
        after, before = rows(from_high, (), x), rows(from_low, (), x)
        free = whole_rows(7, x, after, before)
        freeb[x] = free
        for c in range(3):
            basis[1, c, x] = whole_rows(c, x, after, before)
            basis[0, c, x] = whole_rows(3 + c, x, after, before) * free
        basis[2, 0, x] = whole_rows(6, x, after, before)

    loop(nx, unpack)

    def next_z(v):
        return pltpu.roll(v, width - 1, 1)

    def last_z(v):
        return pltpu.roll(v, 1, 1)

    def next_y(v):
        return pltpu.roll(v, ny - 1, 0)

    def last_y(v):
        return pltpu.roll(v, 1, 0)

    def spread(j, masked):
        def plane(x):
            for c in range(3):
                v = basis[j, c, x]
                if masked:
                    v = v * freeb[x]
                moved = next_z(v)
                total, change = v + moved, moved - v
                shifted = next_y(total)
                nodal[3 * c, x] = total + shifted
                nodal[3 * c + 1, x] = shifted - total
                nodal[3 * c + 2, x] = change + next_y(change)

        loop(nx, plane)

    tiles = [(8 * a, 128 * b) for a in range(ny // 8) for b in range(width // 128)]

    def gradient(e, r, l):
        at = (pl.ds(r, 8), pl.ds(l, 128))
        grad = []
        for c in range(3):
            one = [nodal[(3 * c + d, e) + at] for d in range(3)]
            two = [nodal[(3 * c + d, e + 1) + at] for d in range(3)]
            grad.append([two[0] - one[0], two[1] + one[1], two[2] + one[2]])
        return grad

    pairs = [(0, 0), (0, 1), (0, 2), (1, 1), (1, 2), (2, 2)]

    spread(1, False)

    def build(e):
        for r, l in tiles:
            at = (pl.ds(r, 8), pl.ds(l, 128))
            grad = gradient(e, r, l)
            material = basis[(2, 0, e) + at]
            yy = r + lax.broadcasted_iota(jnp.int32, (8, 128), 0)
            zz = l + lax.broadcasted_iota(jnp.int32, (8, 128), 1)
            zz = jnp.where(zz < sz + STRIP, zz, zz - width)
            zg = zz + gz * sz
            valid = (yy <= ny - 2) & (zz >= -STRIP) & (zz <= sz + STRIP - 2)
            valid = valid & (zg >= 0) & (zg <= nz - 2)
            zero = jnp.zeros((8, 128), jnp.float32)
            lame, shear, mass = zero, zero, zero
            for row in range(table_ref.shape[0]):
                hit = material == float(row)
                lame = jnp.where(hit, table_ref[row, 0], lame)
                shear = jnp.where(hit, table_ref[row, 1], shear)
                mass = jnp.where(hit, table_ref[row, 2], mass)
            lame = jnp.where(valid, lame * 0.0625, 0.0)
            shear = jnp.where(valid, shear * 0.0625, 0.0)
            image[(0, 0, e) + at] = jnp.where(valid, mass * 0.125, 0.0)
            frame = [
                [0.25 * grad[i][j] + (1.0 if i == j else 0.0) for j in range(3)] for i in range(3)
            ]
            strain = {}
            for i, j in pairs:
                v = sum(frame[k][i] * frame[k][j] for k in range(3))
                strain[i, j] = 0.5 * (v - 1.0 if i == j else v)
            bulk = lame * (strain[0, 0] + strain[1, 1] + strain[2, 2])
            for i in range(3):
                for j in range(3):
                    state[(3 * i + j, e) + at] = frame[i][j]
            for place, (i, j) in enumerate(pairs):
                v = 2.0 * shear * strain[i, j]
                state[(9 + place, e) + at] = v + bulk if i == j else v
            state[(15, e) + at] = lame
            state[(16, e) + at] = shear

    loop(nx - 1, build)

    image[0, 0, nx - 1] = jnp.zeros((ny, width), jnp.float32)
    massb[0] = image[0, 0, 0]
    loop(nx - 1, lambda x: massb.__setitem__(x + 1, image[0, 0, x + 1] + image[0, 0, x]))

    def lump(x):
        v = massb[x]
        v = v + last_y(v)
        massb[x] = v + last_z(v)

    loop(nx, lump)

    def apply(j):
        spread(j, True)

        def stress(e):
            for r, l in tiles:
                at = (pl.ds(r, 8), pl.ds(l, 128))
                g = gradient(e, r, l)
                f = [[state[(3 * i + k, e) + at] for k in range(3)] for i in range(3)]
                pulled = [
                    [sum(f[k][a] * g[k][b] for k in range(3)) for b in range(3)] for a in range(3)
                ]
                lame, shear = state[(15, e) + at], state[(16, e) + at]
                bulk = lame * (pulled[0][0] + pulled[1][1] + pulled[2][2])
                t, s = {}, {}
                for place, (a, b) in enumerate(pairs):
                    v = shear * (pulled[a][b] + pulled[b][a])
                    t[a, b] = t[b, a] = v + bulk if a == b else v
                    s[a, b] = s[b, a] = state[(9 + place, e) + at]
                for i in range(3):
                    for b in range(3):
                        v = sum(f[i][k] * t[k, b] for k in range(3))
                        w = sum(g[i][k] * s[k, b] for k in range(3))
                        piola[(3 * i + b, e + 1) + at] = v + w

        loop(nx - 1, stress)

        def gather(x):
            free = freeb[x]
            fixed = 1.0 - free
            for c in range(3):
                across = piola[3 * c, x] - piola[3 * c, x + 1]
                along = piola[3 * c + 1, x] + piola[3 * c + 1, x + 1]
                up = piola[3 * c + 2, x] + piola[3 * c + 2, x + 1]
                flat = (across + last_y(across)) + (last_y(along) - along)
                up = up + last_y(up)
                v = basis[j, c, x]
                out = last_z(flat + up) + (flat - up) + massb[x] * (free * v)
                out = free * out + fixed * v
                image[j, c, x] = out
                if j < 2:
                    basis[j + 1, c, x] = (out - SHIFTS[j] * v) * (1.0 / HALF_WIDTH)

        loop(nx, gather)

    def inner(o):
        entries = [(i, j) for i in range(3) for j in range(3)]

        def plane(x, acc):
            acc = list(acc)
            for c in range(3):
                for r in range(ny // 8):
                    for l in range(sz // 128):
                        at = (pl.ds(8 * r, 8), pl.ds(128 * l, 128))
                        b = [basis[(i, c, x) + at] for i in range(3)]
                        m = [image[(i, c, x) + at] for i in range(3)]
                        for k, (i, j) in enumerate(entries):
                            acc[k] = acc[k] + b[i] * m[j]
                        for i in range(3):
                            acc[9 + i] = acc[9 + i] + b[i] * b[0]
            return tuple(acc)

        acc = tuple(jnp.zeros((8, 128), jnp.float32) for k in range(12))
        if nx <= 8:
            for x in range(nx):
                acc = plane(x, acc)
        else:
            acc = lax.fori_loop(0, nx, plane, acc)
        for k in range(12):
            sums[o, gz, k : k + 1, :] = jnp.sum(acc[k], axis=0, keepdims=True)
        sums[o, gz, 12:ROWS, :] = jnp.zeros((ROWS - 12, 128), jnp.float32)
        for k in range(1, ngz):
            pltpu.make_async_remote_copy(
                src_ref=sums.at[o, gz],
                dst_ref=sums.at[o, gz],
                send_sem=sum_send.at[o],
                recv_sem=sum_recv.at[o],
                device_id={"gx": gx, "gy": gy, "gz": lax.rem(gz + k, ngz)},
                device_id_type=MESH,
            ).start()

    def coefficients(o):
        settle(sums.at[o, pl.ds(0, ngz - 1)], sum_recv.at[o])
        total = sums[o, 0]
        for z in range(1, ngz):
            total = total + sums[o, z]
        total = jnp.sum(total, axis=1, keepdims=True)
        value = [total[k : k + 1, :] for k in range(12)]
        return solve_small([value[0:3], value[3:6], value[6:9]], value[9:12])

    def cut(slot, ref, j):
        for i in range(sx):
            for c in range(3):
                v = ref[j, c, gx * sx + i][:, :sz]
                for g in range(ngy):
                    own[slot, c, i, g] = v[g * sy : (g + 1) * sy]

    for o in range(OUTER):
        for j in range(3):
            apply(j)
        inner(o)
        for j in range(3):
            cut(j, basis, j)
            if o == OUTER - 1:
                cut(3 + j, image, j)
        coeffs = coefficients(o)
        for c in range(3):
            for i in range(sx):
                mine = [own[k, c, i, gy] for k in range(6 if o == OUTER - 1 else 3)]
                gain = coeffs[0] * mine[0] + coeffs[1] * mine[1] + coeffs[2] * mine[2]
                inc_ref[c, i] = gain if o == 0 else inc_ref[c, i] + gain
                if o == OUTER - 1:
                    res_ref[c, i] = mine[0] - (
                        coeffs[0] * mine[3] + coeffs[1] * mine[4] + coeffs[2] * mine[5]
                    )
        if o < OUTER - 1:

            def update(x):
                for c in range(3):
                    basis[0, c, x] = basis[0, c, x] - (
                        coeffs[0] * image[0, c, x]
                        + coeffs[1] * image[1, c, x]
                        + coeffs[2] * image[2, c, x]
                    )

            loop(nx, update)

    settle(blocks.at[pl.ds(0, n - 1)], send_sem.at[0])
    when(has_high, lambda: settle(from_low, send_sem.at[1]))
    when(has_low, lambda: settle(from_high, send_sem.at[2]))
    for o in range(OUTER):
        settle(sums.at[o, pl.ds(0, ngz - 1)], sum_send.at[o])


def per_device(displacement, load, material, free_node, table):
    shard = displacement.shape[1:]
    sx, sy, sz = shard
    grid = tuple(lax.axis_size(a) for a in ("gx", "gy", "gz"))
    n = grid[0] * grid[1]
    nx, ny, width = grid[0] * sx, grid[1] * sy, sz + 128
    f32 = jnp.float32
    out = jax.ShapeDtypeStruct(displacement.shape, f32)
    vmem = pl.BlockSpec(memory_space=pltpu.VMEM)
    return pl.pallas_call(
        functools.partial(kernel, grid, shard),
        out_shape=(out, out),
        in_specs=[vmem] * 4 + [pl.BlockSpec(memory_space=pltpu.SMEM)],
        out_specs=(vmem, vmem),
        scratch_shapes=[
            pltpu.VMEM((n, FIELDS, sx, sy, sz), f32),
            pltpu.VMEM((n, sx, sy, 128), f32),
            pltpu.VMEM((n, sx, sy, 128), f32),
            pltpu.VMEM((sx, sy, 128), f32),
            pltpu.VMEM((sx, sy, 128), f32),
            pltpu.VMEM((3, 3, nx, ny, width), f32),
            pltpu.VMEM((3, 3, nx, ny, width), f32),
            pltpu.VMEM((9, nx, ny, width), f32),
            pltpu.VMEM((9, nx + 1, ny, width), f32),
            pltpu.VMEM((17, nx - 1, ny, width), f32),
            pltpu.VMEM((nx, ny, width), f32),
            pltpu.VMEM((nx, ny, width), f32),
            pltpu.VMEM((6, 3, sx, grid[1], sy, sz), f32),
            pltpu.VMEM((OUTER, grid[2], ROWS, 128), f32),
            pltpu.SemaphoreType.DMA((3,)),
            pltpu.SemaphoreType.DMA((3,)),
            pltpu.SemaphoreType.DMA((OUTER,)),
            pltpu.SemaphoreType.DMA((OUTER,)),
        ],
        compiler_params=pltpu.CompilerParams(
            collective_id=0, has_side_effects=True, vmem_limit_bytes=67043328
        ),
    )(displacement, load, material, free_node, table)


def solution(mesh):
    in_specs = (
        P(None, "gx", "gy", "gz"),
        P(None, "gx", "gy", "gz"),
        P("gx", "gy", "gz"),
        P("gx", "gy", "gz"),
        P(),
    )
    out_specs = (P(None, "gx", "gy", "gz"), P(None, "gx", "gy", "gz"))
    return jax.shard_map(
        per_device, mesh=mesh, in_specs=in_specs, out_specs=out_specs, check_vma=False
    )
```

```python
import functools

import jax
import jax.numpy as jnp
from jax import lax
from jax.experimental import pallas as pl
from jax.experimental.pallas import tpu as pltpu
from jax.sharding import PartitionSpec as P

OUTER = 2
SHIFTS = (9.6, 51.4)
HALF_WIDTH = 29.5
FIELDS = 8
STRIP = 16
ROWS = 16
MESH = pl.DeviceIdType.MESH


def loop(count, body):
    if count <= 8:
        for i in range(count):
            body(i)
    else:

        def step(i, carry):
            body(i)
            return carry

        lax.fori_loop(0, count, step, 0)


def when(condition, body):
    pl.when(condition)(body)


def solve_small(gram, right):
    sym = [[0.5 * (gram[i][j] + gram[j][i]) for j in range(3)] for i in range(3)]
    l00 = jnp.sqrt(sym[0][0])
    l10 = sym[1][0] / l00
    l20 = sym[2][0] / l00
    l11 = jnp.sqrt(sym[1][1] - l10 * l10)
    l21 = (sym[2][1] - l20 * l10) / l11
    l22 = jnp.sqrt(sym[2][2] - l20 * l20 - l21 * l21)
    y0 = right[0] / l00
    y1 = (right[1] - l10 * y0) / l11
    y2 = (right[2] - l20 * y0 - l21 * y1) / l22
    c2 = y2 / l22
    c1 = (y1 - l21 * c2) / l11
    c0 = (y0 - l10 * c1 - l20 * c2) / l00
    return [c0, c1, c2]


def kernel(
    grid,
    shard,
    disp_hbm,
    load_hbm,
    mat_hbm,
    free_hbm,
    table_hbm,
    inc_ref,
    res_ref,
    blocks,
    from_low,
    from_high,
    to_low,
    to_high,
    basis,
    image,
    nodal,
    piola,
    state,
    freeb,
    massb,
    own,
    sums,
    flags,
    table_ref,
    in_sem,
    send_sem,
    recv_sem,
    sum_send,
    sum_recv,
):
    ngx, ngy, ngz = grid
    sx, sy, sz = shard
    nx, ny, nz = ngx * sx, ngy * sy, ngz * sz
    width = sz + 128
    n = ngx * ngy
    gx, gy, gz = lax.axis_index("gx"), lax.axis_index("gy"), lax.axis_index("gz")
    me = gx * ngy + gy
    has_low, has_high = gz > 0, gz < ngz - 1

    def target(p, z):
        return {"gx": p // ngy, "gy": lax.rem(p, ngy), "gz": z}

    def fetch(src, dst, slot):
        return pltpu.make_async_copy(src, dst, in_sem.at[slot])

    fetched = [
        fetch(disp_hbm, blocks.at[me, pl.ds(0, 3)], 0),
        fetch(load_hbm, blocks.at[me, pl.ds(3, 3)], 1),
        fetch(mat_hbm, flags.at[0], 2),
        fetch(free_hbm, flags.at[1], 3),
        fetch(table_hbm, table_ref, 4),
    ]
    for copy in fetched:
        copy.start()

    barrier = pltpu.get_barrier_semaphore()

    def greet(p, z):
        pl.semaphore_signal(barrier, inc=1, device_id=target(p, z), device_id_type=MESH)

    def peers(count, first, body):
        loop(count, lambda k: body(lax.rem(me + first + k, n)))

    peers(n - 1, 1, lambda p: greet(p, gz))
    when(has_low, lambda: peers(n, 0, lambda p: greet(p, gz - 1)))
    when(has_high, lambda: peers(n, 0, lambda p: greet(p, gz + 1)))
    for z in range(ngz):
        when((z > gz + 1) | (z < gz - 1), lambda z=z: greet(me, z))

    for copy in fetched[:4]:
        copy.wait()
    blocks[me, 6] = flags[0].astype(jnp.float32)
    blocks[me, 7] = flags[1].astype(jnp.float32)
    lane = lax.broadcasted_iota(jnp.int32, (sy, 128), 1)
    for i in range(sx):
        low = jnp.zeros((sy, 128), jnp.float32)
        high = jnp.zeros((sy, 128), jnp.float32)
        for f in range(FIELDS):
            part = blocks[me, f, i]
            here = (lane >= STRIP * f) & (lane < STRIP * (f + 1))
            first, last = part[:, :128], part[:, sz - 128 :]
            if f:
                first = pltpu.roll(first, STRIP * f, 1)
            if f < 7:
                last = pltpu.roll(last, STRIP * f + STRIP, 1)
            low = jnp.where(here, first, low)
            high = jnp.where(here, last, high)
        to_low[i] = low
        to_high[i] = high

    def clear(ref):
        ref[...] = jnp.zeros(ref.shape, jnp.float32)

    when(jnp.logical_not(has_low), lambda: clear(from_low))
    when(jnp.logical_not(has_high), lambda: clear(from_high))

    expected = n - 1 + jnp.where(has_low, n, 0) + jnp.where(has_high, n, 0)
    for z in range(ngz):
        expected = expected + jnp.where((z > gz + 1) | (z < gz - 1), 1, 0)
    pl.semaphore_wait(barrier, expected)

    def send(src, dst, slot, p, z):
        pltpu.make_async_remote_copy(
            src_ref=src,
            dst_ref=dst,
            send_sem=send_sem.at[slot],
            recv_sem=recv_sem.at[slot],
            device_id=target(p, z),
            device_id_type=MESH,
        ).start()

    peers(n - 1, 1, lambda p: send(blocks.at[me], blocks.at[me], 0, p, gz))
    when(
        has_high,
        lambda: peers(n, 0, lambda p: send(to_high, from_low.at[me], 1, p, gz + 1)),
    )
    when(
        has_low,
        lambda: peers(n, 0, lambda p: send(to_low, from_high.at[me], 2, p, gz - 1)),
    )

    def settle(ref, sem):
        pltpu.make_async_copy(ref, ref, sem).wait()

    for e in range(9):
        piola[e, 0] = jnp.zeros((ny, width), jnp.float32)
        piola[e, nx] = jnp.zeros((ny, width), jnp.float32)

    settle(blocks.at[pl.ds(0, n - 1)], recv_sem.at[0])
    when(has_low, lambda: settle(from_low, recv_sem.at[1]))
    when(has_high, lambda: settle(from_high, recv_sem.at[2]))

    tail = lax.broadcasted_iota(jnp.int32, (ny, 128), 1)

    def rows(ref, index, x):
        gi, i = x // sx, lax.rem(x, sx) if not isinstance(x, int) else x % sx
        return jnp.concatenate([ref[(gi * ngy + g,) + index + (i,)] for g in range(ngy)], axis=0)

    def whole_rows(f, x, after, before):
        up = after if f == 0 else pltpu.roll(after, 128 - STRIP * f, 1)
        down = before if f == 7 else pltpu.roll(before, 128 - STRIP - STRIP * f, 1)
        halo = jnp.where(tail < STRIP, up, jnp.where(tail >= 128 - STRIP, down, 0.0))
        return jnp.concatenate([rows(blocks, (f,), x), halo], axis=1)

    def unpack(x):
        after, before = rows(from_high, (), x), rows(from_low, (), x)
        free = whole_rows(7, x, after, before)
        freeb[x] = free
        for c in range(3):
            basis[1, c, x] = whole_rows(c, x, after, before)
            basis[0, c, x] = whole_rows(3 + c, x, after, before) * free
        basis[2, 0, x] = whole_rows(6, x, after, before)

    loop(nx, unpack)

    def next_z(v):
        return pltpu.roll(v, width - 1, 1)

    def last_z(v):
        return pltpu.roll(v, 1, 1)

    def next_y(v):
        return pltpu.roll(v, ny - 1, 0)

    def last_y(v):
        return pltpu.roll(v, 1, 0)

    def spread(j, masked):
        def plane(x):
            for c in range(3):
                v = basis[j, c, x]
                if masked:
                    v = v * freeb[x]
                moved = next_z(v)
                total, change = v + moved, moved - v
                shifted = next_y(total)
                nodal[3 * c, x] = total + shifted
                nodal[3 * c + 1, x] = shifted - total
                nodal[3 * c + 2, x] = change + next_y(change)

        loop(nx, plane)

    tiles = [(8 * a, 128 * b) for a in range(ny // 8) for b in range(width // 128)]

    def gradient(e, r, l):
        at = (pl.ds(r, 8), pl.ds(l, 128))
        grad = []
        for c in range(3):
            one = [nodal[(3 * c + d, e) + at] for d in range(3)]
            two = [nodal[(3 * c + d, e + 1) + at] for d in range(3)]
            grad.append([two[0] - one[0], two[1] + one[1], two[2] + one[2]])
        return grad

    pairs = [(0, 0), (0, 1), (0, 2), (1, 1), (1, 2), (2, 2)]

    spread(1, False)
    fetched[4].wait()

    def build(e):
        for r, l in tiles:
            at = (pl.ds(r, 8), pl.ds(l, 128))
            grad = gradient(e, r, l)
            material = basis[(2, 0, e) + at]
            yy = r + lax.broadcasted_iota(jnp.int32, (8, 128), 0)
            zz = l + lax.broadcasted_iota(jnp.int32, (8, 128), 1)
            zz = jnp.where(zz < sz + STRIP, zz, zz - width)
            zg = zz + gz * sz
            valid = (yy <= ny - 2) & (zz >= -STRIP) & (zz <= sz + STRIP - 2)
            valid = valid & (zg >= 0) & (zg <= nz - 2)
            zero = jnp.zeros((8, 128), jnp.float32)
            lame, shear, mass = zero, zero, zero
            for row in range(table_ref.shape[1]):
                hit = material == float(row)
                lame = jnp.where(hit, table_ref[0, row], lame)
                shear = jnp.where(hit, table_ref[1, row], shear)
                mass = jnp.where(hit, table_ref[2, row], mass)
            lame = jnp.where(valid, lame * 0.0625, 0.0)
            shear = jnp.where(valid, shear * 0.0625, 0.0)
            image[(0, 0, e) + at] = jnp.where(valid, mass * 0.125, 0.0)
            frame = [
                [0.25 * grad[i][j] + (1.0 if i == j else 0.0) for j in range(3)] for i in range(3)
            ]
            strain = {}
            for i, j in pairs:
                v = sum(frame[k][i] * frame[k][j] for k in range(3))
                strain[i, j] = 0.5 * (v - 1.0 if i == j else v)
            bulk = lame * (strain[0, 0] + strain[1, 1] + strain[2, 2])
            for i in range(3):
                for j in range(3):
                    state[(3 * i + j, e) + at] = frame[i][j]
            for place, (i, j) in enumerate(pairs):
                v = 2.0 * shear * strain[i, j]
                state[(9 + place, e) + at] = v + bulk if i == j else v
            state[(15, e) + at] = lame
            state[(16, e) + at] = shear

    loop(nx - 1, build)

    image[0, 0, nx - 1] = jnp.zeros((ny, width), jnp.float32)
    massb[0] = image[0, 0, 0]
    loop(nx - 1, lambda x: massb.__setitem__(x + 1, image[0, 0, x + 1] + image[0, 0, x]))

    def lump(x):
        v = massb[x]
        v = v + last_y(v)
        massb[x] = v + last_z(v)

    loop(nx, lump)

    def apply(j):
        spread(j, True)

        def stress(e):
            for r, l in tiles:
                at = (pl.ds(r, 8), pl.ds(l, 128))
                g = gradient(e, r, l)
                f = [[state[(3 * i + k, e) + at] for k in range(3)] for i in range(3)]
                pulled = [
                    [sum(f[k][a] * g[k][b] for k in range(3)) for b in range(3)] for a in range(3)
                ]
                lame, shear = state[(15, e) + at], state[(16, e) + at]
                bulk = lame * (pulled[0][0] + pulled[1][1] + pulled[2][2])
                t, s = {}, {}
                for place, (a, b) in enumerate(pairs):
                    v = shear * (pulled[a][b] + pulled[b][a])
                    t[a, b] = t[b, a] = v + bulk if a == b else v
                    s[a, b] = s[b, a] = state[(9 + place, e) + at]
                for i in range(3):
                    for b in range(3):
                        v = sum(f[i][k] * t[k, b] for k in range(3))
                        w = sum(g[i][k] * s[k, b] for k in range(3))
                        piola[(3 * i + b, e + 1) + at] = v + w

        loop(nx - 1, stress)

        def gather(x):
            free = freeb[x]
            fixed = 1.0 - free
            for c in range(3):
                across = piola[3 * c, x] - piola[3 * c, x + 1]
                along = piola[3 * c + 1, x] + piola[3 * c + 1, x + 1]
                up = piola[3 * c + 2, x] + piola[3 * c + 2, x + 1]
                flat = last_y(across + along) + (across - along)
                up = up + last_y(up)
                v = basis[j, c, x]
                out = last_z(flat + up) + (flat - up) + massb[x] * v
                out = free * out + fixed * v
                image[j, c, x] = out
                if j < 2:
                    basis[j + 1, c, x] = (out - SHIFTS[j] * v) * (1.0 / HALF_WIDTH)

        loop(nx, gather)

    def inner(o):
        entries = [(i, j) for i in range(3) for j in range(3)]

        def plane(x, acc):
            acc = list(acc)
            for c in range(3):
                for r in range(ny // 8):
                    for l in range(sz // 128):
                        at = (pl.ds(8 * r, 8), pl.ds(128 * l, 128))
                        b = [basis[(i, c, x) + at] for i in range(3)]
                        m = [image[(i, c, x) + at] for i in range(3)]
                        for k, (i, j) in enumerate(entries):
                            acc[k] = acc[k] + b[i] * m[j]
                        for i in range(3):
                            acc[9 + i] = acc[9 + i] + b[i] * b[0]
            return tuple(acc)

        acc = tuple(jnp.zeros((8, 128), jnp.float32) for k in range(12))
        if nx <= 8:
            for x in range(nx):
                acc = plane(x, acc)
        else:
            acc = lax.fori_loop(0, nx, plane, acc)
        for k in range(12):
            sums[o, gz, k : k + 1, :] = jnp.sum(acc[k], axis=0, keepdims=True)
        sums[o, gz, 12:ROWS, :] = jnp.zeros((ROWS - 12, 128), jnp.float32)
        for k in range(1, ngz):
            pltpu.make_async_remote_copy(
                src_ref=sums.at[o, gz],
                dst_ref=sums.at[o, gz],
                send_sem=sum_send.at[o],
                recv_sem=sum_recv.at[o],
                device_id={"gx": gx, "gy": gy, "gz": lax.rem(gz + k, ngz)},
                device_id_type=MESH,
            ).start()

    def coefficients(o):
        settle(sums.at[o, pl.ds(0, ngz - 1)], sum_recv.at[o])
        total = sums[o, 0]
        for z in range(1, ngz):
            total = total + sums[o, z]
        total = jnp.sum(total, axis=1, keepdims=True)
        value = [total[k : k + 1, :] for k in range(12)]
        return solve_small([value[0:3], value[3:6], value[6:9]], value[9:12])

    def cut(slot, ref, j):
        for i in range(sx):
            for c in range(3):
                v = ref[j, c, gx * sx + i][:, :sz]
                for g in range(ngy):
                    own[slot, c, i, g] = v[g * sy : (g + 1) * sy]

    for o in range(OUTER):
        for j in range(3):
            apply(j)
        inner(o)
        for j in range(3):
            cut(j, basis, j)
            if o == OUTER - 1:
                cut(3 + j, image, j)
        coeffs = coefficients(o)
        for c in range(3):
            for i in range(sx):
                mine = [own[k, c, i, gy] for k in range(6 if o == OUTER - 1 else 3)]
                gain = coeffs[0] * mine[0] + coeffs[1] * mine[1] + coeffs[2] * mine[2]
                inc_ref[c, i] = gain if o == 0 else inc_ref[c, i] + gain
                if o == OUTER - 1:
                    res_ref[c, i] = mine[0] - (
                        coeffs[0] * mine[3] + coeffs[1] * mine[4] + coeffs[2] * mine[5]
                    )
        if o < OUTER - 1:

            def update(x):
                for c in range(3):
                    basis[0, c, x] = basis[0, c, x] - (
                        coeffs[0] * image[0, c, x]
                        + coeffs[1] * image[1, c, x]
                        + coeffs[2] * image[2, c, x]
                    )

            loop(nx, update)

    settle(blocks.at[pl.ds(0, n - 1)], send_sem.at[0])
    when(has_high, lambda: settle(from_low, send_sem.at[1]))
    when(has_low, lambda: settle(from_high, send_sem.at[2]))
    for o in range(OUTER):
        settle(sums.at[o, pl.ds(0, ngz - 1)], sum_send.at[o])


def per_device(displacement, load, material, free_node, table):
    shard = displacement.shape[1:]
    sx, sy, sz = shard
    grid = tuple(lax.axis_size(a) for a in ("gx", "gy", "gz"))
    n = grid[0] * grid[1]
    nx, ny, width = grid[0] * sx, grid[1] * sy, sz + 128
    f32 = jnp.float32
    out = jax.ShapeDtypeStruct(displacement.shape, f32)
    vmem = pl.BlockSpec(memory_space=pltpu.VMEM)
    buffers = [
        (n, FIELDS, sx, sy, sz),
        (n, sx, sy, 128),
        (n, sx, sy, 128),
        (sx, sy, 128),
        (sx, sy, 128),
        (3, 3, nx, ny, width),
        (3, 3, nx, ny, width),
        (9, nx, ny, width),
        (9, nx + 1, ny, width),
        (17, nx - 1, ny, width),
        (nx, ny, width),
        (nx, ny, width),
        (6, 3, sx, grid[1], sy, sz),
        (OUTER, grid[2], ROWS, 128),
    ]
    return pl.pallas_call(
        functools.partial(kernel, grid, shard),
        out_shape=(out, out),
        in_specs=[pl.BlockSpec(memory_space=pltpu.HBM)] * 5,
        out_specs=(vmem, vmem),
        scratch_shapes=[
            *(pltpu.VMEM(b, f32) for b in buffers),
            pltpu.VMEM((2, sx, sy, sz), jnp.int32),
            pltpu.SMEM(table.shape[::-1], f32),
            pltpu.SemaphoreType.DMA((5,)),
            pltpu.SemaphoreType.DMA((3,)),
            pltpu.SemaphoreType.DMA((3,)),
            pltpu.SemaphoreType.DMA((OUTER,)),
            pltpu.SemaphoreType.DMA((OUTER,)),
        ],
        compiler_params=pltpu.CompilerParams(
            collective_id=0, has_side_effects=True, vmem_limit_bytes=67043328
        ),
    )(displacement, load, material, free_node, table.T)


def solution(mesh):
    in_specs = (
        P(None, "gx", "gy", "gz"),
        P(None, "gx", "gy", "gz"),
        P("gx", "gy", "gz"),
        P("gx", "gy", "gz"),
        P(),
    )
    out_specs = (P(None, "gx", "gy", "gz"), P(None, "gx", "gy", "gz"))
    return jax.shard_map(
        per_device, mesh=mesh, in_specs=in_specs, out_specs=out_specs, check_vma=False
    )
```

```python
import functools

import jax
import jax.numpy as jnp
from jax import lax
from jax.experimental import pallas as pl
from jax.experimental.pallas import tpu as pltpu
from jax.sharding import PartitionSpec as P

OUTER = 2
SHIFTS = (9.6, 51.4)
HALF_WIDTH = 29.5
CHAIN = SHIFTS + (30.5,) + SHIFTS + (30.5,)
FIELDS = 8
STRIP = 16
ROWS = 16
MESH = pl.DeviceIdType.MESH


def loop(count, body):
    if count <= 8:
        for i in range(count):
            body(i)
    else:

        def step(i, carry):
            body(i)
            return carry

        lax.fori_loop(0, count, step, 0)


def when(condition, body):
    pl.when(condition)(body)


def solve_small(gram, right):
    sym = [[0.5 * (gram[i][j] + gram[j][i]) for j in range(3)] for i in range(3)]
    l00 = jnp.sqrt(sym[0][0])
    l10 = sym[1][0] / l00
    l20 = sym[2][0] / l00
    l11 = jnp.sqrt(sym[1][1] - l10 * l10)
    l21 = (sym[2][1] - l20 * l10) / l11
    l22 = jnp.sqrt(sym[2][2] - l20 * l20 - l21 * l21)
    y0 = right[0] / l00
    y1 = (right[1] - l10 * y0) / l11
    y2 = (right[2] - l20 * y0 - l21 * y1) / l22
    c2 = y2 / l22
    c1 = (y1 - l21 * c2) / l11
    c0 = (y0 - l10 * c1 - l20 * c2) / l00
    return [c0, c1, c2]


def kernel(
    grid,
    shard,
    disp_hbm,
    load_hbm,
    mat_hbm,
    free_hbm,
    table_hbm,
    inc_ref,
    res_ref,
    blocks,
    from_low,
    from_high,
    to_low,
    to_high,
    basis,
    nodal,
    piola,
    state,
    freeb,
    massb,
    own,
    sums,
    flags,
    table_ref,
    in_sem,
    send_sem,
    recv_sem,
    sum_send,
    sum_recv,
):
    ngx, ngy, ngz = grid
    sx, sy, sz = shard
    nx, ny, nz = ngx * sx, ngy * sy, ngz * sz
    width = sz + 128
    n = ngx * ngy
    gx, gy, gz = lax.axis_index("gx"), lax.axis_index("gy"), lax.axis_index("gz")
    me = gx * ngy + gy
    has_low, has_high = gz > 0, gz < ngz - 1

    def target(p, z):
        return {"gx": p // ngy, "gy": lax.rem(p, ngy), "gz": z}

    def fetch(src, dst, slot):
        return pltpu.make_async_copy(src, dst, in_sem.at[slot])

    fetched = [
        fetch(disp_hbm, blocks.at[me, pl.ds(0, 3)], 0),
        fetch(load_hbm, blocks.at[me, pl.ds(3, 3)], 1),
        fetch(mat_hbm, flags.at[0], 2),
        fetch(free_hbm, flags.at[1], 3),
        fetch(table_hbm, table_ref, 4),
    ]
    for copy in fetched:
        copy.start()

    barrier = pltpu.get_barrier_semaphore()

    def greet(p, z):
        pl.semaphore_signal(barrier, inc=1, device_id=target(p, z), device_id_type=MESH)

    def peers(count, first, body):
        loop(count, lambda k: body(lax.rem(me + first + k, n)))

    peers(n - 1, 1, lambda p: greet(p, gz))
    when(has_low, lambda: peers(n, 0, lambda p: greet(p, gz - 1)))
    when(has_high, lambda: peers(n, 0, lambda p: greet(p, gz + 1)))
    for z in range(ngz):
        when((z > gz + 1) | (z < gz - 1), lambda z=z: greet(me, z))

    for copy in fetched[:4]:
        copy.wait()
    blocks[me, 6] = flags[0].astype(jnp.float32)
    blocks[me, 7] = flags[1].astype(jnp.float32)
    lane = lax.broadcasted_iota(jnp.int32, (sy, 128), 1)
    for i in range(sx):
        low = jnp.zeros((sy, 128), jnp.float32)
        high = jnp.zeros((sy, 128), jnp.float32)
        for f in range(FIELDS):
            part = blocks[me, f, i]
            here = (lane >= STRIP * f) & (lane < STRIP * (f + 1))
            first, last = part[:, :128], part[:, sz - 128 :]
            if f:
                first = pltpu.roll(first, STRIP * f, 1)
            if f < 7:
                last = pltpu.roll(last, STRIP * f + STRIP, 1)
            low = jnp.where(here, first, low)
            high = jnp.where(here, last, high)
        to_low[i] = low
        to_high[i] = high

    def clear(ref):
        ref[...] = jnp.zeros(ref.shape, jnp.float32)

    when(jnp.logical_not(has_low), lambda: clear(from_low))
    when(jnp.logical_not(has_high), lambda: clear(from_high))

    expected = n - 1 + jnp.where(has_low, n, 0) + jnp.where(has_high, n, 0)
    for z in range(ngz):
        expected = expected + jnp.where((z > gz + 1) | (z < gz - 1), 1, 0)
    pl.semaphore_wait(barrier, expected)

    def send(src, dst, slot, p, z):
        pltpu.make_async_remote_copy(
            src_ref=src,
            dst_ref=dst,
            send_sem=send_sem.at[slot],
            recv_sem=recv_sem.at[slot],
            device_id=target(p, z),
            device_id_type=MESH,
        ).start()

    peers(n - 1, 1, lambda p: send(blocks.at[me], blocks.at[me], 0, p, gz))
    when(
        has_high,
        lambda: peers(n, 0, lambda p: send(to_high, from_low.at[me], 1, p, gz + 1)),
    )
    when(
        has_low,
        lambda: peers(n, 0, lambda p: send(to_low, from_high.at[me], 2, p, gz - 1)),
    )

    def settle(ref, sem):
        pltpu.make_async_copy(ref, ref, sem).wait()

    for e in range(9):
        piola[e, 0] = jnp.zeros((ny, width), jnp.float32)
        piola[e, nx] = jnp.zeros((ny, width), jnp.float32)

    settle(blocks.at[pl.ds(0, n - 1)], recv_sem.at[0])
    when(has_low, lambda: settle(from_low, recv_sem.at[1]))
    when(has_high, lambda: settle(from_high, recv_sem.at[2]))

    tail = lax.broadcasted_iota(jnp.int32, (ny, 128), 1)

    def rows(ref, index, x):
        gi, i = x // sx, lax.rem(x, sx) if not isinstance(x, int) else x % sx
        return jnp.concatenate([ref[(gi * ngy + g,) + index + (i,)] for g in range(ngy)], axis=0)

    def whole_rows(f, x, after, before):
        up = after if f == 0 else pltpu.roll(after, 128 - STRIP * f, 1)
        down = before if f == 7 else pltpu.roll(before, 128 - STRIP - STRIP * f, 1)
        halo = jnp.where(tail < STRIP, up, jnp.where(tail >= 128 - STRIP, down, 0.0))
        return jnp.concatenate([rows(blocks, (f,), x), halo], axis=1)

    def unpack(x):
        after, before = rows(from_high, (), x), rows(from_low, (), x)
        free = whole_rows(7, x, after, before)
        freeb[x] = free
        for c in range(3):
            basis[1, c, x] = whole_rows(c, x, after, before)
            basis[0, c, x] = whole_rows(3 + c, x, after, before) * free
        basis[2, 0, x] = whole_rows(6, x, after, before)

    loop(nx, unpack)

    def next_z(v):
        return pltpu.roll(v, width - 1, 1)

    def last_z(v):
        return pltpu.roll(v, 1, 1)

    def next_y(v):
        return pltpu.roll(v, ny - 1, 0)

    def last_y(v):
        return pltpu.roll(v, 1, 0)

    def spread(j, masked):
        def plane(x):
            for c in range(3):
                v = basis[j, c, x]
                if masked:
                    v = v * freeb[x]
                moved = next_z(v)
                total, change = v + moved, moved - v
                shifted = next_y(total)
                nodal[3 * c, x] = total + shifted
                nodal[3 * c + 1, x] = shifted - total
                nodal[3 * c + 2, x] = change + next_y(change)

        loop(nx, plane)

    tiles = [(8 * a, 128 * b) for a in range(ny // 8) for b in range(width // 128)]

    def gradient(e, r, l):
        at = (pl.ds(r, 8), pl.ds(l, 128))
        grad = []
        for c in range(3):
            one = [nodal[(3 * c + d, e) + at] for d in range(3)]
            two = [nodal[(3 * c + d, e + 1) + at] for d in range(3)]
            grad.append([two[0] - one[0], two[1] + one[1], two[2] + one[2]])
        return grad

    pairs = [(0, 0), (0, 1), (0, 2), (1, 1), (1, 2), (2, 2)]

    spread(1, False)
    fetched[4].wait()

    def build(e):
        for r, l in tiles:
            at = (pl.ds(r, 8), pl.ds(l, 128))
            grad = gradient(e, r, l)
            material = basis[(2, 0, e) + at]
            yy = r + lax.broadcasted_iota(jnp.int32, (8, 128), 0)
            zz = l + lax.broadcasted_iota(jnp.int32, (8, 128), 1)
            zz = jnp.where(zz < sz + STRIP, zz, zz - width)
            zg = zz + gz * sz
            valid = (yy <= ny - 2) & (zz >= -STRIP) & (zz <= sz + STRIP - 2)
            valid = valid & (zg >= 0) & (zg <= nz - 2)
            zero = jnp.zeros((8, 128), jnp.float32)
            lame, shear, mass = zero, zero, zero
            for row in range(table_ref.shape[1]):
                hit = material == float(row)
                lame = jnp.where(hit, table_ref[0, row], lame)
                shear = jnp.where(hit, table_ref[1, row], shear)
                mass = jnp.where(hit, table_ref[2, row], mass)
            lame = jnp.where(valid, lame * 0.0625, 0.0)
            shear = jnp.where(valid, shear * 0.0625, 0.0)
            basis[(3, 0, e) + at] = jnp.where(valid, mass * 0.125, 0.0)
            frame = [
                [0.25 * grad[i][j] + (1.0 if i == j else 0.0) for j in range(3)] for i in range(3)
            ]
            strain = {}
            for i, j in pairs:
                v = sum(frame[k][i] * frame[k][j] for k in range(3))
                strain[i, j] = 0.5 * (v - 1.0 if i == j else v)
            bulk = lame * (strain[0, 0] + strain[1, 1] + strain[2, 2])
            for i in range(3):
                for j in range(3):
                    state[(3 * i + j, e) + at] = frame[i][j]
            for place, (i, j) in enumerate(pairs):
                v = 2.0 * shear * strain[i, j]
                state[(9 + place, e) + at] = v + bulk if i == j else v
            state[(15, e) + at] = lame
            state[(16, e) + at] = shear

    loop(nx - 1, build)

    basis[3, 0, nx - 1] = jnp.zeros((ny, width), jnp.float32)
    massb[0] = basis[3, 0, 0]
    loop(nx - 1, lambda x: massb.__setitem__(x + 1, basis[3, 0, x + 1] + basis[3, 0, x]))

    def lump(x):
        v = massb[x]
        v = v + last_y(v)
        massb[x] = v + last_z(v)

    loop(nx, lump)

    def apply(j):
        spread(j, True)

        def stress(e):
            for r, l in tiles:
                at = (pl.ds(r, 8), pl.ds(l, 128))
                g = gradient(e, r, l)
                f = [[state[(3 * i + k, e) + at] for k in range(3)] for i in range(3)]
                pulled = [
                    [sum(f[k][a] * g[k][b] for k in range(3)) for b in range(3)] for a in range(3)
                ]
                lame, shear = state[(15, e) + at], state[(16, e) + at]
                bulk = lame * (pulled[0][0] + pulled[1][1] + pulled[2][2])
                t, s = {}, {}
                for place, (a, b) in enumerate(pairs):
                    v = shear * (pulled[a][b] + pulled[b][a])
                    t[a, b] = t[b, a] = v + bulk if a == b else v
                    s[a, b] = s[b, a] = state[(9 + place, e) + at]
                for i in range(3):
                    for b in range(3):
                        v = sum(f[i][k] * t[k, b] for k in range(3))
                        w = sum(g[i][k] * s[k, b] for k in range(3))
                        piola[(3 * i + b, e + 1) + at] = v + w

        loop(nx - 1, stress)

        def gather(x):
            free = freeb[x]
            fixed = 1.0 - free
            for c in range(3):
                across = piola[3 * c, x] - piola[3 * c, x + 1]
                along = piola[3 * c + 1, x] + piola[3 * c + 1, x + 1]
                up = piola[3 * c + 2, x] + piola[3 * c + 2, x + 1]
                flat = last_y(across + along) + (across - along)
                up = up + last_y(up)
                v = basis[j, c, x]
                out = last_z(flat + up) + (flat - up) + massb[x] * v
                out = free * out + fixed * v
                basis[j + 1, c, x] = (out - CHAIN[j] * v) * (1.0 / HALF_WIDTH)

        loop(nx, gather)

    def times(coords):
        out = [None] * 7
        for k in range(7):
            if coords[k] is not None:
                out[k] = add(out[k], CHAIN[k] * coords[k])
                out[k + 1] = add(out[k + 1], HALF_WIDTH * coords[k])
        return out

    def add(p, q):
        return q if p is None else p if q is None else p + q

    def scaled(factor, coords):
        return [None if q is None else factor * q for q in coords]

    def plus(p, q):
        return [add(u, w) for u, w in zip(p, q)]

    def combine(coords, vectors):
        return sum(q * w for q, w in zip(coords, vectors) if q is not None)

    def krylov(start):
        b, m = [start], []
        for j in range(3):
            m.append(times(b[j]))
            if j < 2:
                b.append(
                    scaled(1.0 / HALF_WIDTH, plus(m[j], scaled(-SHIFTS[j], b[j])))
                )
        return b, m

    def inner(o, start, images):
        entries = [(i, j) for i in range(3) for j in range(3)]
        if o:
            wide = [
                [None if q is None else jnp.broadcast_to(q, (8, 128)) for q in coords]
                for coords in [start] + images
            ]

        def plane(x, acc):
            acc = list(acc)
            for c in range(3):
                for r in range(ny // 8):
                    for l in range(sz // 128):
                        at = (pl.ds(8 * r, 8), pl.ds(128 * l, 128))
                        v = [basis[(k, c, x) + at] for k in range(7 if o else 4)]
                        if o:
                            b = [combine(wide[0], v)]
                            m = [combine(wide[1 + j], v) for j in range(3)]
                            for j in range(2):
                                b.append((m[j] - SHIFTS[j] * b[j]) * (1.0 / HALF_WIDTH))
                        else:
                            b = v[:3]
                            m = [HALF_WIDTH * v[j + 1] + CHAIN[j] * v[j] for j in range(3)]
                        for k, (i, j) in enumerate(entries):
                            acc[k] = acc[k] + b[i] * m[j]
                        for i in range(3):
                            acc[9 + i] = acc[9 + i] + b[i] * b[0]
            return tuple(acc)

        acc = tuple(jnp.zeros((8, 128), jnp.float32) for k in range(12))
        if nx <= 8:
            for x in range(nx):
                acc = plane(x, acc)
        else:
            acc = lax.fori_loop(0, nx, plane, acc)
        for k in range(12):
            sums[o, gz, k : k + 1, :] = jnp.sum(acc[k], axis=0, keepdims=True)
        sums[o, gz, 12:ROWS, :] = jnp.zeros((ROWS - 12, 128), jnp.float32)
        for k in range(1, ngz):
            pltpu.make_async_remote_copy(
                src_ref=sums.at[o, gz],
                dst_ref=sums.at[o, gz],
                send_sem=sum_send.at[o],
                recv_sem=sum_recv.at[o],
                device_id={"gx": gx, "gy": gy, "gz": lax.rem(gz + k, ngz)},
                device_id_type=MESH,
            ).start()

    def coefficients(o):
        settle(sums.at[o, pl.ds(0, ngz - 1)], sum_recv.at[o])
        total = sums[o, 0]
        for z in range(1, ngz):
            total = total + sums[o, z]
        total = jnp.sum(total, axis=1, keepdims=True)
        value = [total[k : k + 1, :] for k in range(12)]
        return solve_small([value[0:3], value[3:6], value[6:9]], value[9:12])

    for j in range(3):
        apply(j)
    inner(0, None, None)
    for j in range(3, 6):
        apply(j)
    coeffs = coefficients(0)
    one = jnp.ones((1, 1), jnp.float32)
    b, m = krylov([one] + [None] * 6)
    start, gain = b[0], [None] * 7
    for j in range(3):
        gain = plus(gain, scaled(coeffs[j], b[j]))
        start = plus(start, scaled(-coeffs[j], m[j]))
    b, m = krylov(start)
    inner(1, start, m)
    coeffs = coefficients(1)
    left = start
    for j in range(3):
        gain = plus(gain, scaled(coeffs[j], b[j]))
        left = plus(left, scaled(-coeffs[j], m[j]))
    for slot, coords, out_ref in ((0, gain, inc_ref), (1, left, res_ref)):
        for c in range(3):
            for i in range(sx):
                x = gx * sx + i
                v = combine(coords, [basis[k, c, x, :, pl.ds(0, sz)] for k in range(7)])
                for g in range(ngy):
                    own[slot, c, i, g] = v[g * sy : (g + 1) * sy]
                out_ref[c, i] = own[slot, c, i, gy]

    settle(blocks.at[pl.ds(0, n - 1)], send_sem.at[0])
    when(has_high, lambda: settle(from_low, send_sem.at[1]))
    when(has_low, lambda: settle(from_high, send_sem.at[2]))
    for o in range(OUTER):
        settle(sums.at[o, pl.ds(0, ngz - 1)], sum_send.at[o])


def per_device(displacement, load, material, free_node, table):
    shard = displacement.shape[1:]
    sx, sy, sz = shard
    grid = tuple(lax.axis_size(a) for a in ("gx", "gy", "gz"))
    n = grid[0] * grid[1]
    nx, ny, width = grid[0] * sx, grid[1] * sy, sz + 128
    f32 = jnp.float32
    out = jax.ShapeDtypeStruct(displacement.shape, f32)
    vmem = pl.BlockSpec(memory_space=pltpu.VMEM)
    buffers = [
        (n, FIELDS, sx, sy, sz),
        (n, sx, sy, 128),
        (n, sx, sy, 128),
        (sx, sy, 128),
        (sx, sy, 128),
        (7, 3, nx, ny, width),
        (9, nx, ny, width),
        (9, nx + 1, ny, width),
        (17, nx - 1, ny, width),
        (nx, ny, width),
        (nx, ny, width),
        (2, 3, sx, grid[1], sy, sz),
        (OUTER, grid[2], ROWS, 128),
    ]
    return pl.pallas_call(
        functools.partial(kernel, grid, shard),
        out_shape=(out, out),
        in_specs=[pl.BlockSpec(memory_space=pltpu.HBM)] * 5,
        out_specs=(vmem, vmem),
        scratch_shapes=[
            *(pltpu.VMEM(b, f32) for b in buffers),
            pltpu.VMEM((2, sx, sy, sz), jnp.int32),
            pltpu.SMEM(table.shape[::-1], f32),
            pltpu.SemaphoreType.DMA((5,)),
            pltpu.SemaphoreType.DMA((3,)),
            pltpu.SemaphoreType.DMA((3,)),
            pltpu.SemaphoreType.DMA((OUTER,)),
            pltpu.SemaphoreType.DMA((OUTER,)),
        ],
        compiler_params=pltpu.CompilerParams(
            collective_id=0, has_side_effects=True, vmem_limit_bytes=67043328
        ),
    )(displacement, load, material, free_node, table.T)


def solution(mesh):
    in_specs = (
        P(None, "gx", "gy", "gz"),
        P(None, "gx", "gy", "gz"),
        P("gx", "gy", "gz"),
        P("gx", "gy", "gz"),
        P(),
    )
    out_specs = (P(None, "gx", "gy", "gz"), P(None, "gx", "gy", "gz"))
    return jax.shard_map(
        per_device, mesh=mesh, in_specs=in_specs, out_specs=out_specs, check_vma=False
    )
```

```python
import functools

import jax
import jax.numpy as jnp
from jax import lax
from jax.experimental import pallas as pl
from jax.experimental.pallas import tpu as pltpu
from jax.sharding import PartitionSpec as P

OUTER = 2
SHIFTS = (9.6, 51.4)
HALF_WIDTH = 29.5
CHAIN = SHIFTS + (30.5,) + SHIFTS + (30.5,)
FIELDS = 8
FIRST = 5
STRIP = 16
ROWS = 16
MESH = pl.DeviceIdType.MESH


def loop(count, body):
    if count <= 8:
        for i in range(count):
            body(i)
    else:

        def step(i, carry):
            body(i)
            return carry

        lax.fori_loop(0, count, step, 0)


def when(condition, body):
    pl.when(condition)(body)


def solve_small(gram, right):
    sym = [[0.5 * (gram[i][j] + gram[j][i]) for j in range(3)] for i in range(3)]
    l00 = jnp.sqrt(sym[0][0])
    l10 = sym[1][0] / l00
    l20 = sym[2][0] / l00
    l11 = jnp.sqrt(sym[1][1] - l10 * l10)
    l21 = (sym[2][1] - l20 * l10) / l11
    l22 = jnp.sqrt(sym[2][2] - l20 * l20 - l21 * l21)
    y0 = right[0] / l00
    y1 = (right[1] - l10 * y0) / l11
    y2 = (right[2] - l20 * y0 - l21 * y1) / l22
    c2 = y2 / l22
    c1 = (y1 - l21 * c2) / l11
    c0 = (y0 - l10 * c1 - l20 * c2) / l00
    return [c0, c1, c2]


def kernel(
    grid,
    shard,
    disp_hbm,
    load_hbm,
    mat_hbm,
    free_hbm,
    table_hbm,
    inc_ref,
    res_ref,
    blocks,
    from_low,
    from_high,
    to_low,
    to_high,
    basis,
    nodal,
    piola,
    state,
    freeb,
    massb,
    own,
    sums,
    flags,
    table_ref,
    in_sem,
    send_sem,
    recv_sem,
    sum_send,
    sum_recv,
):
    ngx, ngy, ngz = grid
    sx, sy, sz = shard
    nx, ny, nz = ngx * sx, ngy * sy, ngz * sz
    width = sz + 128
    n = ngx * ngy
    gx, gy, gz = lax.axis_index("gx"), lax.axis_index("gy"), lax.axis_index("gz")
    me = gx * ngy + gy
    has_low, has_high = gz > 0, gz < ngz - 1

    def target(p, z):
        return {"gx": p // ngy, "gy": lax.rem(p, ngy), "gz": z}

    def fetch(src, dst, slot):
        return pltpu.make_async_copy(src, dst, in_sem.at[slot])

    fetched = [
        fetch(disp_hbm, blocks.at[me, pl.ds(0, 3)], 0),
        fetch(load_hbm, blocks.at[me, pl.ds(FIRST, 3)], 1),
        fetch(mat_hbm, flags.at[0], 2),
        fetch(free_hbm, flags.at[1], 3),
        fetch(table_hbm, table_ref, 4),
    ]
    for copy in fetched:
        copy.start()

    barrier = pltpu.get_barrier_semaphore()

    def greet(p, z):
        pl.semaphore_signal(barrier, inc=1, device_id=target(p, z), device_id_type=MESH)

    def peers(count, first, body):
        loop(count, lambda k: body(lax.rem(me + first + k, n)))

    when(has_low, lambda: peers(n, 0, lambda p: greet(p, gz - 1)))
    when(has_high, lambda: peers(n, 0, lambda p: greet(p, gz + 1)))
    for z in range(ngz):
        when((z > gz + 1) | (z < gz - 1), lambda z=z: greet(me, z))
    peers(n - 1, 1, lambda p: greet(p, gz))

    for copy in fetched[:4]:
        copy.wait()
    blocks[me, 3] = flags[0].astype(jnp.float32)
    blocks[me, 4] = flags[1].astype(jnp.float32)
    lane = lax.broadcasted_iota(jnp.int32, (sy, 128), 1)
    for i in range(sx):
        low = jnp.zeros((sy, 128), jnp.float32)
        high = jnp.zeros((sy, 128), jnp.float32)
        for f in range(FIELDS):
            part = blocks[me, f, i]
            here = (lane >= STRIP * f) & (lane < STRIP * (f + 1))
            first, last = part[:, :128], part[:, sz - 128 :]
            if f:
                first = pltpu.roll(first, STRIP * f, 1)
            if f < 7:
                last = pltpu.roll(last, STRIP * f + STRIP, 1)
            low = jnp.where(here, first, low)
            high = jnp.where(here, last, high)
        to_low[i] = low
        to_high[i] = high

    def clear(ref):
        ref[...] = jnp.zeros(ref.shape, jnp.float32)

    when(jnp.logical_not(has_low), lambda: clear(from_low))
    when(jnp.logical_not(has_high), lambda: clear(from_high))

    expected = n - 1 + jnp.where(has_low, n, 0) + jnp.where(has_high, n, 0)
    for z in range(ngz):
        expected = expected + jnp.where((z > gz + 1) | (z < gz - 1), 1, 0)
    pl.semaphore_wait(barrier, expected)

    def send(src, dst, slot, p, z):
        pltpu.make_async_remote_copy(
            src_ref=src,
            dst_ref=dst,
            send_sem=send_sem.at[slot],
            recv_sem=recv_sem.at[slot],
            device_id=target(p, z),
            device_id_type=MESH,
        ).start()

    when(
        has_high,
        lambda: peers(n, 0, lambda p: send(to_high, from_low.at[me], 1, p, gz + 1)),
    )
    when(
        has_low,
        lambda: peers(n, 0, lambda p: send(to_low, from_high.at[me], 2, p, gz - 1)),
    )

    early = blocks.at[me, pl.ds(0, FIRST)]
    late = blocks.at[me, pl.ds(FIRST, FIELDS - FIRST)]
    peers(n - 1, 1, lambda p: send(early, early, 0, p, gz))
    peers(n - 1, 1, lambda p: send(late, late, 3, p, gz))
    early_all = blocks.at[pl.ds(0, n - 1), pl.ds(0, FIRST)]
    late_all = blocks.at[pl.ds(0, n - 1), pl.ds(FIRST, FIELDS - FIRST)]

    def settle(ref, sem):
        pltpu.make_async_copy(ref, ref, sem).wait()

    for e in range(9):
        piola[e, 0] = jnp.zeros((ny, width), jnp.float32)
        piola[e, nx] = jnp.zeros((ny, width), jnp.float32)

    settle(early_all, recv_sem.at[0])
    when(has_low, lambda: settle(from_low, recv_sem.at[1]))
    when(has_high, lambda: settle(from_high, recv_sem.at[2]))

    tail = lax.broadcasted_iota(jnp.int32, (ny, 128), 1)

    def rows(ref, index, x):
        gi, i = x // sx, lax.rem(x, sx) if not isinstance(x, int) else x % sx
        return jnp.concatenate([ref[(gi * ngy + g,) + index + (i,)] for g in range(ngy)], axis=0)

    def whole_rows(f, x, after, before):
        up = after if f == 0 else pltpu.roll(after, 128 - STRIP * f, 1)
        down = before if f == 7 else pltpu.roll(before, 128 - STRIP - STRIP * f, 1)
        halo = jnp.where(tail < STRIP, up, jnp.where(tail >= 128 - STRIP, down, 0.0))
        return jnp.concatenate([rows(blocks, (f,), x), halo], axis=1)

    def unpack(x):
        after, before = rows(from_high, (), x), rows(from_low, (), x)
        freeb[x] = whole_rows(4, x, after, before)
        for c in range(3):
            basis[1, c, x] = whole_rows(c, x, after, before)
        basis[2, 0, x] = whole_rows(3, x, after, before)

    loop(nx, unpack)

    def next_z(v):
        return pltpu.roll(v, width - 1, 1)

    def last_z(v):
        return pltpu.roll(v, 1, 1)

    def next_y(v):
        return pltpu.roll(v, ny - 1, 0)

    def last_y(v):
        return pltpu.roll(v, 1, 0)

    def spread(j, masked):
        def plane(x):
            for c in range(3):
                v = basis[j, c, x]
                if masked:
                    v = v * freeb[x]
                moved = next_z(v)
                total, change = v + moved, moved - v
                shifted = next_y(total)
                nodal[3 * c, x] = total + shifted
                nodal[3 * c + 1, x] = shifted - total
                nodal[3 * c + 2, x] = change + next_y(change)

        loop(nx, plane)

    tiles = [(8 * a, 128 * b) for a in range(ny // 8) for b in range(width // 128)]

    def gradient(e, r, l):
        at = (pl.ds(r, 8), pl.ds(l, 128))
        grad = []
        for c in range(3):
            one = [nodal[(3 * c + d, e) + at] for d in range(3)]
            two = [nodal[(3 * c + d, e + 1) + at] for d in range(3)]
            grad.append([two[0] - one[0], two[1] + one[1], two[2] + one[2]])
        return grad

    pairs = [(0, 0), (0, 1), (0, 2), (1, 1), (1, 2), (2, 2)]

    spread(1, False)
    fetched[4].wait()

    def build(e):
        for r, l in tiles:
            at = (pl.ds(r, 8), pl.ds(l, 128))
            grad = gradient(e, r, l)
            material = basis[(2, 0, e) + at]
            yy = r + lax.broadcasted_iota(jnp.int32, (8, 128), 0)
            zz = l + lax.broadcasted_iota(jnp.int32, (8, 128), 1)
            zz = jnp.where(zz < sz + STRIP, zz, zz - width)
            zg = zz + gz * sz
            valid = (yy <= ny - 2) & (zz >= -STRIP) & (zz <= sz + STRIP - 2)
            valid = valid & (zg >= 0) & (zg <= nz - 2)
            zero = jnp.zeros((8, 128), jnp.float32)
            lame, shear, mass = zero, zero, zero
            for row in range(table_ref.shape[1]):
                hit = material == float(row)
                lame = jnp.where(hit, table_ref[0, row], lame)
                shear = jnp.where(hit, table_ref[1, row], shear)
                mass = jnp.where(hit, table_ref[2, row], mass)
            lame = jnp.where(valid, lame * 0.0625, 0.0)
            shear = jnp.where(valid, shear * 0.0625, 0.0)
            basis[(3, 0, e) + at] = jnp.where(valid, mass * 0.125, 0.0)
            frame = [
                [0.25 * grad[i][j] + (1.0 if i == j else 0.0) for j in range(3)] for i in range(3)
            ]
            strain = {}
            for i, j in pairs:
                v = sum(frame[k][i] * frame[k][j] for k in range(3))
                strain[i, j] = 0.5 * (v - 1.0 if i == j else v)
            bulk = lame * (strain[0, 0] + strain[1, 1] + strain[2, 2])
            for i in range(3):
                for j in range(3):
                    state[(3 * i + j, e) + at] = frame[i][j]
            for place, (i, j) in enumerate(pairs):
                v = 2.0 * shear * strain[i, j]
                state[(9 + place, e) + at] = v + bulk if i == j else v
            state[(15, e) + at] = lame
            state[(16, e) + at] = shear

    loop(nx - 1, build)

    basis[3, 0, nx - 1] = jnp.zeros((ny, width), jnp.float32)
    massb[0] = basis[3, 0, 0]
    loop(nx - 1, lambda x: massb.__setitem__(x + 1, basis[3, 0, x + 1] + basis[3, 0, x]))

    def lump(x):
        v = massb[x]
        v = v + last_y(v)
        massb[x] = v + last_z(v)

    loop(nx, lump)

    def apply(j):
        spread(j, True)

        def stress(e):
            for r, l in tiles:
                at = (pl.ds(r, 8), pl.ds(l, 128))
                g = gradient(e, r, l)
                f = [[state[(3 * i + k, e) + at] for k in range(3)] for i in range(3)]
                pulled = [
                    [sum(f[k][a] * g[k][b] for k in range(3)) for b in range(3)] for a in range(3)
                ]
                lame, shear = state[(15, e) + at], state[(16, e) + at]
                bulk = lame * (pulled[0][0] + pulled[1][1] + pulled[2][2])
                t, s = {}, {}
                for place, (a, b) in enumerate(pairs):
                    v = shear * (pulled[a][b] + pulled[b][a])
                    t[a, b] = t[b, a] = v + bulk if a == b else v
                    s[a, b] = s[b, a] = state[(9 + place, e) + at]
                for i in range(3):
                    for b in range(3):
                        v = sum(f[i][k] * t[k, b] for k in range(3))
                        w = sum(g[i][k] * s[k, b] for k in range(3))
                        piola[(3 * i + b, e + 1) + at] = v + w

        loop(nx - 1, stress)

        def gather(x):
            free = freeb[x]
            fixed = 1.0 - free
            for c in range(3):
                across = piola[3 * c, x] - piola[3 * c, x + 1]
                along = piola[3 * c + 1, x] + piola[3 * c + 1, x + 1]
                up = piola[3 * c + 2, x] + piola[3 * c + 2, x + 1]
                flat = last_y(across + along) + (across - along)
                up = up + last_y(up)
                v = basis[j, c, x]
                out = last_z(flat + up) + (flat - up) + massb[x] * v
                out = free * out + fixed * v
                basis[j + 1, c, x] = (out - CHAIN[j] * v) * (1.0 / HALF_WIDTH)

        loop(nx, gather)

    def times(coords):
        out = [None] * 7
        for k in range(7):
            if coords[k] is not None:
                out[k] = add(out[k], CHAIN[k] * coords[k])
                out[k + 1] = add(out[k + 1], HALF_WIDTH * coords[k])
        return out

    def add(p, q):
        return q if p is None else p if q is None else p + q

    def scaled(factor, coords):
        return [None if q is None else factor * q for q in coords]

    def plus(p, q):
        return [add(u, w) for u, w in zip(p, q)]

    def combine(coords, vectors):
        return sum(q * w for q, w in zip(coords, vectors) if q is not None)

    def krylov(start):
        b, m = [start], []
        for j in range(3):
            m.append(times(b[j]))
            if j < 2:
                b.append(
                    scaled(1.0 / HALF_WIDTH, plus(m[j], scaled(-SHIFTS[j], b[j])))
                )
        return b, m

    def inner(o, start, images):
        entries = [(i, j) for i in range(3) for j in range(3)]
        if o:
            wide = [
                [None if q is None else jnp.broadcast_to(q, (8, 128)) for q in coords]
                for coords in [start] + images
            ]

        def plane(x, acc):
            acc = list(acc)
            for c in range(3):
                for r in range(ny // 8):
                    for l in range(sz // 128):
                        at = (pl.ds(8 * r, 8), pl.ds(128 * l, 128))
                        v = [basis[(k, c, x) + at] for k in range(7 if o else 4)]
                        if o:
                            b = [combine(wide[0], v)]
                            m = [combine(wide[1 + j], v) for j in range(3)]
                            for j in range(2):
                                b.append((m[j] - SHIFTS[j] * b[j]) * (1.0 / HALF_WIDTH))
                        else:
                            b = v[:3]
                            m = [HALF_WIDTH * v[j + 1] + CHAIN[j] * v[j] for j in range(3)]
                        for k, (i, j) in enumerate(entries):
                            acc[k] = acc[k] + b[i] * m[j]
                        for i in range(3):
                            acc[9 + i] = acc[9 + i] + b[i] * b[0]
            return tuple(acc)

        acc = tuple(jnp.zeros((8, 128), jnp.float32) for k in range(12))
        if nx <= 8:
            for x in range(nx):
                acc = plane(x, acc)
        else:
            acc = lax.fori_loop(0, nx, plane, acc)
        for k in range(12):
            sums[o, gz, k : k + 1, :] = jnp.sum(acc[k], axis=0, keepdims=True)
        sums[o, gz, 12:ROWS, :] = jnp.zeros((ROWS - 12, 128), jnp.float32)
        for k in range(1, ngz):
            pltpu.make_async_remote_copy(
                src_ref=sums.at[o, gz],
                dst_ref=sums.at[o, gz],
                send_sem=sum_send.at[o],
                recv_sem=sum_recv.at[o],
                device_id={"gx": gx, "gy": gy, "gz": lax.rem(gz + k, ngz)},
                device_id_type=MESH,
            ).start()

    def coefficients(o):
        settle(sums.at[o, pl.ds(0, ngz - 1)], sum_recv.at[o])
        total = sums[o, 0]
        for z in range(1, ngz):
            total = total + sums[o, z]
        total = jnp.sum(total, axis=1, keepdims=True)
        value = [total[k : k + 1, :] for k in range(12)]
        return solve_small([value[0:3], value[3:6], value[6:9]], value[9:12])

    settle(late_all, recv_sem.at[3])

    def begin(x):
        after, before = rows(from_high, (), x), rows(from_low, (), x)
        for c in range(3):
            basis[0, c, x] = freeb[x] * whole_rows(FIRST + c, x, after, before)

    loop(nx, begin)

    for j in range(3):
        apply(j)
    inner(0, None, None)
    for j in range(3, 6):
        apply(j)
    coeffs = coefficients(0)
    one = jnp.ones((1, 1), jnp.float32)
    b, m = krylov([one] + [None] * 6)
    start, gain = b[0], [None] * 7
    for j in range(3):
        gain = plus(gain, scaled(coeffs[j], b[j]))
        start = plus(start, scaled(-coeffs[j], m[j]))
    b, m = krylov(start)
    inner(1, start, m)
    coeffs = coefficients(1)
    left = start
    for j in range(3):
        gain = plus(gain, scaled(coeffs[j], b[j]))
        left = plus(left, scaled(-coeffs[j], m[j]))
    for slot, coords, out_ref in ((0, gain, inc_ref), (1, left, res_ref)):
        for c in range(3):
            for i in range(sx):
                x = gx * sx + i
                v = combine(coords, [basis[k, c, x, :, pl.ds(0, sz)] for k in range(7)])
                for g in range(ngy):
                    own[slot, c, i, g] = v[g * sy : (g + 1) * sy]
                out_ref[c, i] = own[slot, c, i, gy]

    settle(early_all, send_sem.at[0])
    settle(late_all, send_sem.at[3])
    when(has_high, lambda: settle(from_low, send_sem.at[1]))
    when(has_low, lambda: settle(from_high, send_sem.at[2]))
    for o in range(OUTER):
        settle(sums.at[o, pl.ds(0, ngz - 1)], sum_send.at[o])


def per_device(displacement, load, material, free_node, table):
    shard = displacement.shape[1:]
    sx, sy, sz = shard
    grid = tuple(lax.axis_size(a) for a in ("gx", "gy", "gz"))
    n = grid[0] * grid[1]
    nx, ny, width = grid[0] * sx, grid[1] * sy, sz + 128
    f32 = jnp.float32
    out = jax.ShapeDtypeStruct(displacement.shape, f32)
    vmem = pl.BlockSpec(memory_space=pltpu.VMEM)
    buffers = [
        (n, FIELDS, sx, sy, sz),
        (n, sx, sy, 128),
        (n, sx, sy, 128),
        (sx, sy, 128),
        (sx, sy, 128),
        (7, 3, nx, ny, width),
        (9, nx, ny, width),
        (9, nx + 1, ny, width),
        (17, nx - 1, ny, width),
        (nx, ny, width),
        (nx, ny, width),
        (2, 3, sx, grid[1], sy, sz),
        (OUTER, grid[2], ROWS, 128),
    ]
    return pl.pallas_call(
        functools.partial(kernel, grid, shard),
        out_shape=(out, out),
        in_specs=[pl.BlockSpec(memory_space=pltpu.HBM)] * 5,
        out_specs=(vmem, vmem),
        scratch_shapes=[
            *(pltpu.VMEM(b, f32) for b in buffers),
            pltpu.VMEM((2, sx, sy, sz), jnp.int32),
            pltpu.SMEM(table.shape[::-1], f32),
            pltpu.SemaphoreType.DMA((5,)),
            pltpu.SemaphoreType.DMA((4,)),
            pltpu.SemaphoreType.DMA((4,)),
            pltpu.SemaphoreType.DMA((OUTER,)),
            pltpu.SemaphoreType.DMA((OUTER,)),
        ],
        compiler_params=pltpu.CompilerParams(
            collective_id=0, has_side_effects=True, vmem_limit_bytes=67043328
        ),
    )(displacement, load, material, free_node, table.T)


def solution(mesh):
    in_specs = (
        P(None, "gx", "gy", "gz"),
        P(None, "gx", "gy", "gz"),
        P("gx", "gy", "gz"),
        P("gx", "gy", "gz"),
        P(),
    )
    out_specs = (P(None, "gx", "gy", "gz"), P(None, "gx", "gy", "gz"))
    return jax.shard_map(
        per_device, mesh=mesh, in_specs=in_specs, out_specs=out_specs, check_vma=False
    )
```
